256 devices in a mesh: doc: 8 (over y, core), term: 32 (over x, z).
Axes of the slice: x: 4, y: 4, z: 8, core: 2. Of those that a mesh axis runs over, the one named last changes fastest.
Arguments:
- slab: float32 [8192, 32768], P('doc', 'term'), may hold values from 0.05 to 4
- doc_factor: float32 [8192, 128], P('doc'), may hold values from 0.02 to 5, as said below
- term_factor: float32 [32768, 128], P('term'), may hold values from 0.005 to 5, as said below
Outputs:
- doc_out: float32 [8192, 128], P('doc')
- term_out: float32 [32768, 128], P('term')
The draws below stay inside these ranges and needn't reach their ends.
Inputs may be any that keep to these rules, and one draw needn't show every extreme that they name: `doc_factor`: positive entries. `term_factor`: positive entries.
All inputs are finite; a program needn't handle non-finite values.
Results may differ from the reference program's by a relative error of at most 0.0001.
Values sent between devices are 32-bit elements; how exact they have to be, the bound alone decides.
No kernel may reach another device: no remote copies, remote signals or barrier semaphores. Data moves between devices by JAX's collectives and lax.ppermute only.
A program may use at most 64 MiB of HBM per device.

```python
import math
import jax
import jax.numpy as jnp
from jax import lax

RANK = 128
OUTER = 2
INNER = 2
DOCS = 8192
TERMS = 32768


def peaked_rows(key, count, width, low, high):
    first = jax.random.fold_in(key, 1)
    second = jax.random.fold_in(key, 2)
    third = jax.random.fold_in(key, 3)
    base = jnp.exp(jax.random.uniform(first, (count, width), jnp.float32, math.log(low), math.log(high)))
    peak = jnp.exp(jax.random.uniform(third, (count,), jnp.float32, 0.0, math.log(5.0)))
    topic = jax.random.randint(second, (count,), 0, width)
    chosen = jnp.arange(width)[None, :] == topic[:, None]
    return jnp.where(chosen, peak[:, None], base).astype(jnp.float32)


def draw_doc_factor(key, part):
    return peaked_rows(jax.random.fold_in(key, 11), DOCS, RANK, 0.02, 0.2)


def draw_term_factor(key, part):
    return peaked_rows(jax.random.fold_in(key, 23), TERMS, RANK, 0.005, 0.05)


def shard_levels(rng, extent, shards, low, largest):
    level, own = 1.0, jax.random.fold_in(rng, 6)
    for axis_at, blocks in shards:
        draws = jnp.exp(jax.random.uniform(jax.random.fold_in(own, axis_at), (blocks,), jnp.float32, low / len(shards), largest / len(shards)))
        level = level * jnp.repeat(draws, extent[axis_at] // blocks).reshape([-1 if axis == axis_at else 1 for axis in range(len(extent))])
    return level


def setup_inputs(seed: int = 0) -> dict:
    keys = jax.random.split(jax.random.key(seed), 4)
    return {
        "slab": jnp.clip(jnp.exp(math.log(4.0) - 4.3820266 * jax.random.uniform(keys[0], (DOCS, TERMS), jnp.float32) ** shard_levels(keys[0], (DOCS, TERMS), ((0, 8), (1, 32)), -0.2, 0.2)), 0.05, 4.0),
        "doc_factor": draw_doc_factor(jax.random.fold_in(keys[3], 71), 0),
        "term_factor": draw_term_factor(jax.random.fold_in(keys[3], 71), 0),
    }


def quotient(slab, doc_factor, term_factor):
    product = jnp.dot(doc_factor, term_factor.T, precision=lax.Precision.HIGHEST, preferred_element_type=jnp.float32)
    return slab / product


def reference(slab, doc_factor, term_factor):
    for _ in range(OUTER):
        for _ in range(INNER):
            ratios = quotient(slab, doc_factor, term_factor)
            numerator = jnp.dot(ratios, term_factor, precision=lax.Precision.HIGHEST, preferred_element_type=jnp.float32)
            doc_factor = doc_factor * numerator / jnp.sum(term_factor, axis=0)
        ratios = quotient(slab, doc_factor, term_factor)
        numerator = jnp.dot(ratios.T, doc_factor, precision=lax.Precision.HIGHEST, preferred_element_type=jnp.float32)
        term_factor = term_factor * numerator / jnp.sum(doc_factor, axis=0)
    return doc_factor, term_factor
```

```python
import jax
import jax.numpy as jnp
from jax import lax
from jax.sharding import Mesh, PartitionSpec as P

OUTER = 2
INNER = 2
NEAR = ("x", "zl")
FAR = "zh"
DOC = ("y", "core")
TERM = ("x", "zh", "zl")


def exchange(blocks, axis):
    return lax.all_to_all(blocks, axis, split_axis=0, concat_axis=0, tiled=True)


def spread(value, axis):
    return exchange(jnp.broadcast_to(value, (lax.axis_size(axis), *value.shape)), axis)


def dot(a, b, dims):
    return lax.dot_general(
        a, b, (dims, ((), ())), precision=lax.Precision.HIGH, preferred_element_type=jnp.float32
    )


def with_row(blocks, row):
    extra = jnp.zeros((blocks.shape[0], 8, blocks.shape[2]), blocks.dtype)
    extra = extra.at[:, 0, :].set(row)
    return jnp.concatenate([blocks, extra], axis=1)


def own_slice(value, axis):
    rows = value.shape[0] // lax.axis_size(axis)
    return lax.dynamic_slice_in_dim(value, lax.axis_index(axis) * rows, rows, 0)


def on_device(slab, doc_factor, term_factor):
    near, across = lax.axis_size(NEAR), lax.axis_size(DOC)
    rank = doc_factor.shape[1]
    docs = doc_factor.shape[0] // near
    terms = term_factor.shape[0] // across
    doc_own = own_slice(doc_factor, NEAR)
    term_own = own_slice(term_factor, DOC)
    for _ in range(OUTER):
        for inner in range(INNER):
            ratios = slab / dot(doc_factor, term_factor, ((1,), (1,)))
            partial = dot(ratios, term_factor, ((1,), (0,)))
            blocks = partial.reshape(near, docs, rank)
            if inner == 0:
                blocks = with_row(blocks, jnp.sum(term_factor, axis=0))
            share = jnp.sum(exchange(blocks, NEAR), axis=0)
            share = jnp.sum(spread(share, FAR), axis=0)
            if inner == 0:
                term_mass = share[docs]
            doc_own = doc_own * share[:docs] / term_mass
            doc_factor = spread(doc_own, NEAR).reshape(-1, rank)
        ratios = slab / dot(doc_factor, term_factor, ((1,), (1,)))
        partial = dot(ratios, doc_factor, ((0,), (0,)))
        blocks = with_row(partial.reshape(across, terms, rank), jnp.sum(doc_factor, axis=0))
        share = jnp.sum(exchange(blocks, DOC), axis=0)
        term_own = term_own * share[:terms] / share[terms]
        term_factor = spread(term_own, DOC).reshape(-1, rank)
    return (doc_factor, term_factor)


def solution(mesh):
    parts = Mesh(mesh.devices.reshape(4, 2, 4, 4, 2), ("y", "core", "x", "zh", "zl"))
    return jax.shard_map(
        on_device,
        mesh=parts,
        in_specs=(P(DOC, TERM), P(DOC, None), P(TERM, None)),
        out_specs=(P(DOC, None), P(TERM, None)),
        check_vma=False,
    )
```

```python
import functools

import jax
import jax.numpy as jnp
from jax import lax
from jax.experimental import pallas as pl
from jax.experimental.pallas import tpu as pltpu
from jax.sharding import Mesh, PartitionSpec as P

OUTER = 2
INNER = 2
NEAR = ("x", "zl")
FAR = "zh"
DOC = ("y", "core")
TERM = ("x", "zh", "zl")
F32 = jnp.float32
PAD = 8
HELD = 512
DOC_STEP = 256
TERM_STEP = 512
LIMIT = 50


def exchange(blocks, axis):
    return lax.all_to_all(blocks, axis, split_axis=0, concat_axis=0, tiled=True)


def spread(value, axis):
    return exchange(jnp.broadcast_to(value, (lax.axis_size(axis), *value.shape)), axis)


def swap(value, axis, by=1):
    return lax.ppermute(value, axis, [(at, at ^ by) for at in range(lax.axis_size(axis))])


def total_over(value, axis):
    return sum([swap(value, axis, by) for by in range(1, lax.axis_size(axis))], value)


def own_slice(value, axis):
    rows = value.shape[0] // lax.axis_size(axis)
    return lax.dynamic_slice_in_dim(value, lax.axis_index(axis) * rows, rows, 0)


def halves(value):
    high = value.astype(jnp.bfloat16)
    return high, (value - high.astype(F32)).astype(jnp.bfloat16)


def product_of(doc, term_cat):
    high, low = doc
    return lax.dot_general(
        jnp.concatenate([high, low, high, low], axis=1),
        term_cat,
        (((1,), (1,)), ((), ())),
        preferred_element_type=F32,
    )


def term_operand(term):
    high, low = term
    return jnp.concatenate([high, high, low, low], axis=1)


def quotients(first, slab_ref, near_ref, docs, term_cat, held, arrived):
    split, step = near_ref.shape[0], docs[0][0].shape[0]
    head = pltpu.make_async_copy(slab_ref.at[pl.ds(0, split)], near_ref, arrived.at[0])
    tail = pltpu.make_async_copy(
        slab_ref.at[pl.ds(split, held.shape[0])], held, arrived.at[1]
    )
    if first:
        head.start()
    tail.start()
    products = [product_of(doc, term_cat) for doc in docs]
    if first:
        head.wait()
    for at, product in enumerate(products):
        start = at * step
        if start == split:
            tail.wait()
        source = near_ref if start < split else held
        yield halves(source[pl.ds(start % split, step), :] / product)


def doc_blocks(doc_ref, step):
    return [halves(doc_ref[start : start + step, :]) for start in range(0, doc_ref.shape[0], step)]


def doc_kernel(first, mass, slab_ref, near_ref, doc_ref, term_ref, out_ref, held, arrived):
    term = halves(term_ref[...])
    pair = jnp.concatenate(term, axis=1)
    pair = jnp.concatenate([pair, pair], axis=0)
    rank = doc_ref.shape[1]
    rows = out_ref.shape[1] - (PAD if mass else 0)
    docs = doc_blocks(doc_ref, DOC_STEP)
    start = 0
    for quotient in quotients(first, slab_ref, near_ref, docs, term_operand(term), held, arrived):
        both = jnp.dot(jnp.concatenate(quotient, axis=1), pair, preferred_element_type=F32)
        result = both[:, :rank] + both[:, rank:]
        for offset in range(0, DOC_STEP, rows):
            out_ref[(start + offset) // rows, :rows, :] = result[offset : offset + rows, :]
        start += DOC_STEP
    if mass:
        total = jnp.sum(term_ref[...], axis=0, keepdims=True)
        for at in range(out_ref.shape[0]):
            out_ref[at, rows:, :] = jnp.broadcast_to(total, (PAD, rank))


def term_kernel(first, mass, slab_ref, near_ref, doc_ref, term_ref, out_ref, held, arrived):
    rank = doc_ref.shape[1]
    term_cat = term_operand(halves(term_ref[...]))
    docs = doc_blocks(doc_ref, TERM_STEP)
    total = None
    for doc, quotient in zip(docs, quotients(first, slab_ref, near_ref, docs, term_cat, held, arrived)):
        pair = jnp.concatenate(doc, axis=1)
        part = lax.dot_general(
            jnp.concatenate(quotient, axis=0),
            jnp.concatenate([pair, pair], axis=0),
            (((0,), (0,)), ((), ())),
            preferred_element_type=F32,
        )
        total = part if total is None else total + part
    result = total[:, :rank] + total[:, rank:]
    sums = jnp.sum(doc_ref[...], axis=0, keepdims=True)
    count, rows = out_ref.shape[0], out_ref.shape[1] - PAD
    for at in range(count):
        out_ref[at, :rows, :] = result[at * rows : (at + 1) * rows, :]
        out_ref[at, rows:, :] = jnp.broadcast_to(sums, (PAD, rank))


def first_kernel(kernel, mass, slab_ref, doc_ref, term_ref, out_ref, near_ref, held, arrived):
    kernel(True, mass, slab_ref, near_ref, doc_ref, term_ref, out_ref, held, arrived)


def call(kernel, mass, shape, slab, near, doc, term):
    whole = pl.BlockSpec(memory_space=pltpu.VMEM)
    apart = pl.BlockSpec(memory_space=pltpu.HBM)
    first = near is None
    out = jax.ShapeDtypeStruct(shape, F32)
    kept = jax.ShapeDtypeStruct((HELD, slab.shape[1]), F32)
    return pl.pallas_call(
        functools.partial(first_kernel, kernel, mass) if first else functools.partial(kernel, False, mass),
        out_shape=(out, kept) if first else out,
        in_specs=[apart, whole, whole] if first else [apart, whole, whole, whole],
        out_specs=(whole, whole) if first else whole,
        scratch_shapes=[
            pltpu.VMEM((slab.shape[0] - HELD, slab.shape[1]), F32),
            pltpu.SemaphoreType.DMA((2,)),
        ],
        compiler_params=pltpu.CompilerParams(vmem_limit_bytes=LIMIT * 2**20),
    )(*((slab, doc, term) if first else (slab, near, doc, term)))


def on_device(slab, doc_factor, term_factor):
    near = lax.axis_size(NEAR)
    rank = doc_factor.shape[1]
    docs = doc_factor.shape[0] // near
    across = lax.axis_size("y")
    terms = term_factor.shape[0] // (2 * across)
    core, row = (lax.axis_index(axis).astype(jnp.uint32) for axis in ("core", "y"))
    here, away = core * across, (1 - core) * across
    partner = [row ^ at for at in range(across)]
    doc_own = own_slice(doc_factor, NEAR)
    term_own = own_slice(term_factor, ("core", "y"))
    slab, doc_factor, term_factor, doc_own, term_own, core, here, away, partner = lax.optimization_barrier(
        (slab, doc_factor, term_factor, doc_own, term_own, core, here, away, partner)
    )
    held = None
    for _ in range(OUTER):
        for inner in range(INNER):
            mass = inner == 0
            shape = (near, docs + (PAD if mass else 0), rank)
            blocks = call(doc_kernel, mass, shape, slab, held, doc_factor, term_factor)
            if held is None:
                blocks, held = blocks
            share = jnp.sum(exchange(blocks, NEAR), axis=0)
            share = total_over(share, FAR)
            if mass:
                term_mass = share[docs]
            doc_own = doc_own * share[:docs] / term_mass
            doc_factor = spread(doc_own, NEAR).reshape(-1, rank)
        shape = (2 * across, terms + PAD, rank)
        blocks = call(term_kernel, True, shape, slab, held, doc_factor, term_factor)
        mine = lax.dynamic_slice_in_dim(blocks, here, across, 0)
        other = lax.dynamic_slice_in_dim(blocks, away, across, 0)
        mine = mine + swap(other, "core")
        pieces = [lax.dynamic_index_in_dim(mine, at, 0, keepdims=False) for at in partner]
        share = sum([swap(pieces[by], "y", by) for by in range(1, across)], pieces[0])
        term_own = term_own * share[:terms] / share[terms]
        pieces = jnp.stack([term_own] + [swap(term_own, "y", by) for by in range(1, across)])
        mine = jnp.concatenate([lax.dynamic_index_in_dim(pieces, at, 0, keepdims=False) for at in partner], axis=0)
        other = swap(mine, "core")
        first = core == 0
        term_factor = jnp.concatenate(
            [jnp.where(first, mine, other), jnp.where(first, other, mine)], axis=0
        )
    return (doc_factor, term_factor)


def solution(mesh):
    parts = Mesh(mesh.devices.reshape(4, 2, 4, 4, 2), ("y", "core", "x", "zh", "zl"))
    return jax.shard_map(
        on_device,
        mesh=parts,
        in_specs=(P(DOC, TERM), P(DOC, None), P(TERM, None)),
        out_specs=(P(DOC, None), P(TERM, None)),
        check_vma=False,
    )
```

```python
import functools

import jax
import jax.numpy as jnp
from jax import lax
from jax.experimental import pallas as pl
from jax.experimental.pallas import tpu as pltpu
from jax.sharding import Mesh, PartitionSpec as P

OUTER = 2
INNER = 2
NEAR = ("x", "zl")
FAR = "zh"
DOC = ("y", "core")
TERM = ("x", "zh", "zl")
TERM_OWN = ("core", "y")
F32 = jnp.float32
PAD = 8
ORDER = (1, 3, 2)
HELD = 512
DOC_STEP = 256
TERM_STEP = 512
LIMIT = 50


def exchange(blocks, axis):
    return lax.all_to_all(blocks, axis, split_axis=0, concat_axis=0, tiled=True)


def spread(value, axis):
    return exchange(jnp.broadcast_to(value, (lax.axis_size(axis), *value.shape)), axis)


def swap(value, axis, by=1):
    return lax.ppermute(value, axis, [(at, at ^ by) for at in range(lax.axis_size(axis))])


def total_over(value, axis):
    return sum([swap(value, axis, by) for by in ORDER], value)


def halves(value):
    high = value.astype(jnp.bfloat16)
    return high, (value - high.astype(F32)).astype(jnp.bfloat16)


def product_of(doc, term_cat):
    high, low = doc
    return lax.dot_general(
        jnp.concatenate([high, low, high, low], axis=1),
        term_cat,
        (((1,), (1,)), ((), ())),
        preferred_element_type=F32,
    )


def term_operand(term):
    high, low = term
    return jnp.concatenate([high, high, low, low], axis=1)


def quotients(first, slab_ref, near_ref, docs, term_cat, held, arrived):
    split, step = near_ref.shape[0], docs[0][0].shape[0]
    if first:
        head = pltpu.make_async_copy(slab_ref.at[pl.ds(0, split)], near_ref, arrived.at[0])
        head.start()
    tail = pltpu.make_async_copy(
        slab_ref.at[pl.ds(split, held.shape[0])], held, arrived.at[1]
    )
    tail.start()
    products = [product_of(doc, term_cat) for doc in docs]
    if first:
        head.wait()
    for at, product in enumerate(products):
        start = at * step
        if start == split:
            tail.wait()
        source = near_ref if start < split else held
        yield halves(source[pl.ds(start % split, step), :] / product)


def loaded(term_refs):
    if len(term_refs) == 1:
        return term_refs[0][...]
    mine, other = (ref[...] for ref in term_refs)
    first = lax.axis_index("core") == 0
    return jnp.concatenate([jnp.where(first, mine, other), jnp.where(first, other, mine)], axis=0)


def doc_blocks(doc_ref, step):
    return [halves(doc_ref[start : start + step, :]) for start in range(0, doc_ref.shape[0], step)]


def doc_kernel(first, mass, slab_ref, near_ref, doc_ref, term_refs, out_ref, held, arrived):
    term_value = loaded(term_refs)
    term = halves(term_value)
    pair = jnp.concatenate(term, axis=1)
    pair = jnp.concatenate([pair, pair], axis=0)
    rank = doc_ref.shape[1]
    rows = out_ref.shape[1] - (PAD if mass else 0)
    docs = doc_blocks(doc_ref, DOC_STEP)
    start = 0
    for quotient in quotients(first, slab_ref, near_ref, docs, term_operand(term), held, arrived):
        both = jnp.dot(jnp.concatenate(quotient, axis=1), pair, preferred_element_type=F32)
        result = both[:, :rank] + both[:, rank:]
        for offset in range(0, DOC_STEP, rows):
            out_ref[(start + offset) // rows, :rows, :] = result[offset : offset + rows, :]
        start += DOC_STEP
    if mass:
        total = jnp.sum(term_value, axis=0, keepdims=True)
        for at in range(out_ref.shape[0]):
            out_ref[at, rows:, :] = jnp.broadcast_to(total, (PAD, rank))


def term_kernel(slab_ref, near_ref, doc_ref, term_refs, out_ref, held, arrived):
    rank = doc_ref.shape[1]
    term_cat = term_operand(halves(loaded(term_refs)))
    docs = doc_blocks(doc_ref, TERM_STEP)
    total = None
    for doc, quotient in zip(docs, quotients(False, slab_ref, near_ref, docs, term_cat, held, arrived)):
        pair = jnp.concatenate(doc, axis=1)
        part = lax.dot_general(
            jnp.concatenate(quotient, axis=0),
            jnp.concatenate([pair, pair], axis=0),
            (((0,), (0,)), ((), ())),
            preferred_element_type=F32,
        )
        total = part if total is None else total + part
    result = total[:, :rank] + total[:, rank:]
    sums = jnp.sum(doc_ref[...], axis=0, keepdims=True)
    count, rows = out_ref.shape[0], out_ref.shape[1] - PAD
    for at in range(count):
        out_ref[at, :rows, :] = result[at * rows : (at + 1) * rows, :]
        out_ref[at, rows:, :] = jnp.broadcast_to(sums, (PAD, rank))


def first_doc(slab_ref, doc_ref, term_ref, out_ref, near_ref, doc_own, term_own, held, arrived):
    doc_kernel(True, True, slab_ref, near_ref, doc_ref, (term_ref,), out_ref, held, arrived)
    for axis, source, target in ((NEAR, doc_ref, doc_own), (TERM_OWN, term_ref, term_own)):
        rows = target.shape[0]
        start = pl.multiple_of(lax.axis_index(axis) * rows, rows)
        target[...] = source[pl.ds(start, rows), :]


def later_doc(mass, slab_ref, near_ref, doc_ref, *refs):
    *term_refs, out_ref, held, arrived = refs
    doc_kernel(False, mass, slab_ref, near_ref, doc_ref, term_refs, out_ref, held, arrived)


def any_term(last, slab_ref, near_ref, doc_ref, *refs):
    if not last:
        *term_refs, out_ref, held, arrived = refs
        term_kernel(slab_ref, near_ref, doc_ref, term_refs, out_ref, held, arrived)
        return
    *term_refs, out_ref, doc_out, held, arrived = refs
    copy = pltpu.make_async_copy(doc_ref, doc_out, arrived.at[2])
    copy.start()
    term_kernel(slab_ref, near_ref, doc_ref, term_refs, out_ref, held, arrived)
    copy.wait()


WHOLE = pl.BlockSpec(memory_space=pltpu.VMEM)
APART = pl.BlockSpec(memory_space=pltpu.HBM)


def array(*shape):
    return jax.ShapeDtypeStruct(shape, F32)


def call(kernel, arrays, in_specs, outs, out_specs):
    slab = arrays[0]
    return pl.pallas_call(
        kernel,
        out_shape=outs,
        in_specs=in_specs,
        out_specs=out_specs,
        scratch_shapes=[
            pltpu.VMEM((slab.shape[0] - HELD, slab.shape[1]), F32),
            pltpu.SemaphoreType.DMA((3,)),
        ],
        compiler_params=pltpu.CompilerParams(vmem_limit_bytes=LIMIT * 2**20),
    )(*arrays)


def on_device(slab, doc_factor, term_factor):
    near = lax.axis_size(NEAR)
    rank = doc_factor.shape[1]
    docs = doc_factor.shape[0] // near
    across = lax.axis_size("y")
    terms = term_factor.shape[0] // (2 * across)
    core, row = (lax.axis_index(axis).astype(jnp.uint32) for axis in ("core", "y"))
    here, away = core * across, (1 - core) * across
    partner = [row ^ at for at in range(across)]
    slab, doc_factor, term_factor, core, here, away, partner = lax.optimization_barrier(
        (slab, doc_factor, term_factor, core, here, away, partner)
    )
    term_factor = (term_factor,)
    held = None
    for outer in range(OUTER):
        for inner in range(INNER):
            mass = inner == 0
            blocks = array(near, docs + (PAD if mass else 0), rank)
            if held is None:
                blocks, held, doc_own, term_own = call(
                    first_doc,
                    (slab, doc_factor, *term_factor),
                    [APART, WHOLE, WHOLE],
                    (blocks, array(HELD, slab.shape[1]), array(docs, rank), array(terms, rank)),
                    (WHOLE,) * 4,
                )
            else:
                blocks = call(
                    functools.partial(later_doc, mass),
                    (slab, held, doc_factor, *term_factor),
                    [APART] + [WHOLE] * (2 + len(term_factor)),
                    blocks,
                    WHOLE,
                )
            share = jnp.sum(exchange(blocks, NEAR), axis=0)
            share = total_over(share, FAR)
            if mass:
                term_mass = share[docs]
            doc_own = doc_own * share[:docs] / term_mass
            doc_factor = spread(doc_own, NEAR).reshape(-1, rank)
        last = outer == OUTER - 1
        blocks = array(2 * across, terms + PAD, rank)
        blocks = call(
            functools.partial(any_term, last),
            (slab, held, doc_factor, *term_factor),
            [APART] + [WHOLE] * (2 + len(term_factor)),
            (blocks, array(*doc_factor.shape)) if last else blocks,
            (WHOLE, APART) if last else WHOLE,
        )
        if last:
            blocks, doc_factor = blocks
        mine = lax.dynamic_slice_in_dim(blocks, here, across, 0)
        other = lax.dynamic_slice_in_dim(blocks, away, across, 0)
        mine = mine + swap(other, "core")
        pieces = [lax.dynamic_index_in_dim(mine, at, 0, keepdims=False) for at in partner]
        share = sum([swap(pieces[by], "y", by) for by in ORDER], pieces[0])
        term_own = term_own * share[:terms] / share[terms]
        pieces = {by: swap(term_own, "y", by) for by in ORDER}
        pieces = jnp.stack([term_own] + [pieces[by] for by in range(1, across)])
        mine = jnp.concatenate([lax.dynamic_index_in_dim(pieces, at, 0, keepdims=False) for at in partner], axis=0)
        other = swap(mine, "core")
        term_factor = (mine, other)
    first = core == 0
    term_factor = jnp.concatenate([jnp.where(first, mine, other), jnp.where(first, other, mine)], axis=0)
    return (doc_factor, term_factor)


def solution(mesh):
    parts = Mesh(mesh.devices.reshape(4, 2, 4, 4, 2), ("y", "core", "x", "zh", "zl"))
    return jax.shard_map(
        on_device,
        mesh=parts,
        in_specs=(P(DOC, TERM), P(DOC, None), P(TERM, None)),
        out_specs=(P(DOC, None), P(TERM, None)),
        check_vma=False,
    )
```

```python
import functools

import jax
import jax.numpy as jnp
from jax import lax
from jax.experimental import pallas as pl
from jax.experimental.pallas import tpu as pltpu
from jax.sharding import Mesh, PartitionSpec as P

OUTER = 2
INNER = 2
NEAR = ("zl", "x")
FAR = "zh"
DOC = ("y", "core")
TERM = ("x", "zh", "zl")
TERM_OWN = ("core", "y")
F32 = jnp.float32
PAD = 8
ORDER = (3, 1, 2)
SCATTER = (2, 1, 3)
GATHER = (1, 3, 2)
HELD = 512
DOC_STEP = 256
TERM_STEP = 512
LIMIT = 50


def exchange(blocks, axis):
    return lax.all_to_all(blocks, axis, split_axis=0, concat_axis=0, tiled=True)


def spread(value, axis):
    return exchange(jnp.broadcast_to(value, (lax.axis_size(axis), *value.shape)), axis)


def swap(value, axis, by=1):
    return lax.ppermute(value, axis, [(at, at ^ by) for at in range(lax.axis_size(axis))])


def total_over(value, axis):
    return sum([swap(value, axis, by) for by in ORDER], value)


def halves(value):
    high = value.astype(jnp.bfloat16)
    return high, (value - high.astype(F32)).astype(jnp.bfloat16)


def product_of(doc, term_cat):
    high, low = doc
    return lax.dot_general(
        jnp.concatenate([high, low, high, low], axis=1),
        term_cat,
        (((1,), (1,)), ((), ())),
        preferred_element_type=F32,
    )


def term_operand(term):
    high, low = term
    return jnp.concatenate([high, high, low, low], axis=1)


def quotients(first, slab_ref, near_ref, docs, term_cat, held, arrived):
    split, step = near_ref.shape[0], docs[0][0].shape[0]
    if first:
        head = pltpu.make_async_copy(slab_ref.at[pl.ds(0, split)], near_ref, arrived.at[0])
        head.start()
    tail = pltpu.make_async_copy(
        slab_ref.at[pl.ds(split, held.shape[0])], held, arrived.at[1]
    )
    tail.start()
    products = [product_of(doc, term_cat) for doc in docs]
    if first:
        head.wait()
    for at, product in enumerate(products):
        start = at * step
        if start == split:
            tail.wait()
        source = near_ref if start < split else held
        yield halves(source[pl.ds(start % split, step), :] / product)


def loaded(term_refs):
    if len(term_refs) == 1:
        return term_refs[0][...]
    mine, other = (ref[...] for ref in term_refs)
    first = lax.axis_index("core") == 0
    return jnp.concatenate([jnp.where(first, mine, other), jnp.where(first, other, mine)], axis=0)


def doc_blocks(doc_ref, step):
    return [halves(doc_ref[start : start + step, :]) for start in range(0, doc_ref.shape[0], step)]


def doc_kernel(first, mass, slab_ref, near_ref, doc_ref, term_refs, out_ref, held, arrived):
    term_value = loaded(term_refs)
    term = halves(term_value)
    pair = jnp.concatenate(term, axis=1)
    pair = jnp.concatenate([pair, pair], axis=0)
    rank = doc_ref.shape[1]
    rows = out_ref.shape[1] - (PAD if mass else 0)
    docs = doc_blocks(doc_ref, DOC_STEP)
    start = 0
    for quotient in quotients(first, slab_ref, near_ref, docs, term_operand(term), held, arrived):
        both = jnp.dot(jnp.concatenate(quotient, axis=1), pair, preferred_element_type=F32)
        result = both[:, :rank] + both[:, rank:]
        for offset in range(0, DOC_STEP, rows):
            out_ref[(start + offset) // rows, :rows, :] = result[offset : offset + rows, :]
        start += DOC_STEP
    if mass:
        total = jnp.sum(term_value, axis=0, keepdims=True)
        for at in range(out_ref.shape[0]):
            out_ref[at, rows:, :] = jnp.broadcast_to(total, (PAD, rank))


def term_kernel(slab_ref, near_ref, doc_ref, term_refs, out_ref, held, arrived):
    rank = doc_ref.shape[1]
    term_cat = term_operand(halves(loaded(term_refs)))
    docs = doc_blocks(doc_ref, TERM_STEP)
    total = None
    for doc, quotient in zip(docs, quotients(False, slab_ref, near_ref, docs, term_cat, held, arrived)):
        pair = jnp.concatenate(doc, axis=1)
        part = lax.dot_general(
            jnp.concatenate(quotient, axis=0),
            jnp.concatenate([pair, pair], axis=0),
            (((0,), (0,)), ((), ())),
            preferred_element_type=F32,
        )
        total = part if total is None else total + part
    result = total[:, :rank] + total[:, rank:]
    sums = jnp.sum(doc_ref[...], axis=0, keepdims=True)
    count, rows = out_ref.shape[0], out_ref.shape[1] - PAD
    for at in range(count):
        out_ref[at, :rows, :] = result[at * rows : (at + 1) * rows, :]
        out_ref[at, rows:, :] = jnp.broadcast_to(sums, (PAD, rank))


def first_doc(slab_ref, doc_in, term_in, out_ref, near_ref, doc_own, term_own, held, doc_ref, term_ref, arrived):
    copies = [
        pltpu.make_async_copy(term_in, term_ref, arrived.at[2]),
        pltpu.make_async_copy(doc_in, doc_ref, arrived.at[3]),
    ]
    for copy in copies:
        copy.start()
    for copy in copies:
        copy.wait()
    doc_kernel(True, True, slab_ref, near_ref, doc_ref, (term_ref,), out_ref, held, arrived)
    for axis, source, target in ((NEAR, doc_ref, doc_own), (TERM_OWN, term_ref, term_own)):
        rows = target.shape[0]
        start = pl.multiple_of(lax.axis_index(axis) * rows, rows)
        target[...] = source[pl.ds(start, rows), :]


def later_doc(mass, slab_ref, near_ref, doc_ref, *refs):
    *term_refs, out_ref, held, arrived = refs
    doc_kernel(False, mass, slab_ref, near_ref, doc_ref, term_refs, out_ref, held, arrived)


def any_term(last, slab_ref, near_ref, doc_ref, *refs):
    if not last:
        *term_refs, out_ref, held, arrived = refs
        term_kernel(slab_ref, near_ref, doc_ref, term_refs, out_ref, held, arrived)
        return
    *term_refs, out_ref, doc_out, held, arrived = refs
    copy = pltpu.make_async_copy(doc_ref, doc_out, arrived.at[2])
    copy.start()
    term_kernel(slab_ref, near_ref, doc_ref, term_refs, out_ref, held, arrived)
    copy.wait()


WHOLE = pl.BlockSpec(memory_space=pltpu.VMEM)
APART = pl.BlockSpec(memory_space=pltpu.HBM)


def array(*shape):
    return jax.ShapeDtypeStruct(shape, F32)


def call(kernel, arrays, in_specs, outs, out_specs, extra=()):
    slab = arrays[0]
    return pl.pallas_call(
        kernel,
        out_shape=outs,
        in_specs=in_specs,
        out_specs=out_specs,
        scratch_shapes=[
            pltpu.VMEM((slab.shape[0] - HELD, slab.shape[1]), F32),
            *extra,
            pltpu.SemaphoreType.DMA((4,)),
        ],
        compiler_params=pltpu.CompilerParams(vmem_limit_bytes=LIMIT * 2**20),
    )(*arrays)


def on_device(slab, doc_factor, term_factor):
    near = lax.axis_size(NEAR)
    rank = doc_factor.shape[1]
    docs = doc_factor.shape[0] // near
    across = lax.axis_size("y")
    terms = term_factor.shape[0] // (2 * across)
    core, row = (lax.axis_index(axis).astype(jnp.uint32) for axis in ("core", "y"))
    here, away = core * across, (1 - core) * across
    partner = [row ^ at for at in range(across)]
    spots = [at ^ (at >> 1) for at in partner]
    slab, doc_factor, term_factor, core, here, away, partner, spots = lax.optimization_barrier(
        (slab, doc_factor, term_factor, core, here, away, partner, spots)
    )
    term_factor = (term_factor,)
    held = None
    for outer in range(OUTER):
        for inner in range(INNER):
            mass = inner == 0
            blocks = array(near, docs + (PAD if mass else 0), rank)
            if held is None:
                blocks, held, doc_own, term_own = call(
                    first_doc,
                    (slab, *(pltpu.with_memory_space_constraint(factor, pltpu.HBM) for factor in (doc_factor, *term_factor))),
                    [APART] * 3,
                    (blocks, array(HELD, slab.shape[1]), array(docs, rank), array(terms, rank)),
                    (WHOLE,) * 4,
                    [pltpu.VMEM(doc_factor.shape, F32), pltpu.VMEM(term_factor[0].shape, F32)],
                )
            else:
                blocks = call(
                    functools.partial(later_doc, mass),
                    (slab, held, doc_factor, *term_factor),
                    [APART] + [WHOLE] * (2 + len(term_factor)),
                    blocks,
                    WHOLE,
                )
            share = jnp.sum(exchange(blocks, NEAR), axis=0)
            share = total_over(share, FAR)
            if mass:
                term_mass = share[docs]
            doc_own = doc_own * share[:docs] / term_mass
            doc_factor = spread(doc_own, NEAR).reshape(-1, rank)
        last = outer == OUTER - 1
        blocks = array(2 * across, terms + PAD, rank)
        blocks = call(
            functools.partial(any_term, last),
            (slab, held, doc_factor, *term_factor),
            [APART] + [WHOLE] * (2 + len(term_factor)),
            (blocks, array(*doc_factor.shape)) if last else blocks,
            (WHOLE, APART) if last else WHOLE,
        )
        if last:
            blocks, doc_factor = blocks
        mine = lax.dynamic_slice_in_dim(blocks, here, across, 0)
        other = lax.dynamic_slice_in_dim(blocks, away, across, 0)
        mine = mine + swap(other, "core")
        pieces = [lax.dynamic_index_in_dim(mine, at, 0, keepdims=False) for at in partner]
        share = sum([swap(pieces[by], "y", by) for by in SCATTER], pieces[0])
        term_own = term_own * share[:terms] / share[terms]
        pieces = jnp.stack([term_own] + [swap(term_own, "y", by) for by in GATHER])
        mine = jnp.concatenate([lax.dynamic_index_in_dim(pieces, at, 0, keepdims=False) for at in spots], axis=0)
        other = swap(mine, "core")
        term_factor = (mine, other)
    first = core == 0
    term_factor = jnp.concatenate([jnp.where(first, mine, other), jnp.where(first, other, mine)], axis=0)
    return (doc_factor, term_factor)


def solution(mesh):
    parts = Mesh(mesh.devices.reshape(4, 2, 4, 4, 2), ("y", "core", "x", "zh", "zl"))
    return jax.shard_map(
        on_device,
        mesh=parts,
        in_specs=(P(DOC, TERM), P(DOC, None), P(TERM, None)),
        out_specs=(P(DOC, None), P(TERM, None)),
        check_vma=False,
    )
```

```python
import functools

import jax
import jax.numpy as jnp
from jax import lax
from jax.experimental import pallas as pl
from jax.experimental.pallas import tpu as pltpu
from jax.sharding import Mesh, PartitionSpec as P

OUTER = 2
INNER = 2
NEAR = ("zl", "x")
FAR = "zh"
DOC = ("y", "core")
TERM = ("x", "zh", "zl")
TERM_OWN = ("core", "y")
F32 = jnp.float32
PAD = 8
ORDER = (3, 1, 2)
SCATTER = (2, 1, 3)
GATHER = (1, 3, 2)
HELD = 512
DOC_STEP = 256
TERM_STEP = 512
LIMIT = 50


def exchange(blocks, axis):
    return lax.all_to_all(blocks, axis, split_axis=0, concat_axis=0, tiled=True)


def spread(value, axis):
    return exchange(jnp.broadcast_to(value, (lax.axis_size(axis), *value.shape)), axis)


def swap(value, axis, by=1):
    return lax.ppermute(value, axis, [(at, at ^ by) for at in range(lax.axis_size(axis))])


def total_over(value, axis):
    return sum([swap(value, axis, by) for by in ORDER], value)


def halves(value):
    high = value.astype(jnp.bfloat16)
    return high, (value - high.astype(F32)).astype(jnp.bfloat16)


def product_of(doc, term_cat):
    high, low = doc
    return lax.dot_general(
        jnp.concatenate([high, low, high, low], axis=1),
        term_cat,
        (((1,), (1,)), ((), ())),
        preferred_element_type=F32,
    )


def term_operand(term):
    high, low = term
    return jnp.concatenate([high, high, low, low], axis=1)


def head_copy(slab_ref, near_ref, arrived):
    return pltpu.make_async_copy(slab_ref.at[pl.ds(0, HELD)], near_ref, arrived.at[0])


def tail_copy(slab_ref, held, arrived):
    return pltpu.make_async_copy(slab_ref.at[pl.ds(HELD, held.shape[0])], held, arrived.at[1])


def quotients(first, slab_ref, near_ref, docs, term_cat, held, arrived):
    split, step = near_ref.shape[0], docs[0][0].shape[0]
    tail = tail_copy(slab_ref, held, arrived)
    if not first:
        tail.start()
    products = [product_of(doc, term_cat) for doc in docs]
    if first:
        head_copy(slab_ref, near_ref, arrived).wait()
    for at, product in enumerate(products):
        start = at * step
        if start == split:
            tail.wait()
        source = near_ref if start < split else held
        yield halves(source[pl.ds(start % split, step), :] / product)


def loaded(term_refs):
    if len(term_refs) == 1:
        return term_refs[0][...]
    mine, other = (ref[...] for ref in term_refs)
    first = lax.axis_index("core") == 0
    return jnp.concatenate([jnp.where(first, mine, other), jnp.where(first, other, mine)], axis=0)


def doc_blocks(doc_ref, step):
    return [halves(doc_ref[start : start + step, :]) for start in range(0, doc_ref.shape[0], step)]


def doc_kernel(first, mass, slab_ref, near_ref, doc_ref, term_refs, out_ref, held, arrived):
    term_value = loaded(term_refs)
    term = halves(term_value)
    pair = jnp.concatenate(term, axis=1)
    pair = jnp.concatenate([pair, pair], axis=0)
    rank = doc_ref.shape[1]
    rows = out_ref.shape[1] - (PAD if mass else 0)
    docs = doc_blocks(doc_ref, DOC_STEP)
    start = 0
    for quotient in quotients(first, slab_ref, near_ref, docs, term_operand(term), held, arrived):
        both = jnp.dot(jnp.concatenate(quotient, axis=1), pair, preferred_element_type=F32)
        result = both[:, :rank] + both[:, rank:]
        for offset in range(0, DOC_STEP, rows):
            out_ref[(start + offset) // rows, :rows, :] = result[offset : offset + rows, :]
        start += DOC_STEP
    if mass:
        total = jnp.sum(term_value, axis=0, keepdims=True)
        for at in range(out_ref.shape[0]):
            out_ref[at, rows:, :] = jnp.broadcast_to(total, (PAD, rank))


def term_kernel(slab_ref, near_ref, doc_ref, term_refs, out_ref, held, arrived):
    rank = doc_ref.shape[1]
    term_cat = term_operand(halves(loaded(term_refs)))
    docs = doc_blocks(doc_ref, TERM_STEP)
    total = None
    for doc, quotient in zip(docs, quotients(False, slab_ref, near_ref, docs, term_cat, held, arrived)):
        pair = jnp.concatenate(doc, axis=1)
        part = lax.dot_general(
            jnp.concatenate(quotient, axis=0),
            jnp.concatenate([pair, pair], axis=0),
            (((0,), (0,)), ((), ())),
            preferred_element_type=F32,
        )
        total = part if total is None else total + part
    result = total[:, :rank] + total[:, rank:]
    sums = jnp.sum(doc_ref[...], axis=0, keepdims=True)
    count, rows = out_ref.shape[0], out_ref.shape[1] - PAD
    for at in range(count):
        out_ref[at, :rows, :] = result[at * rows : (at + 1) * rows, :]
        out_ref[at, rows:, :] = jnp.broadcast_to(sums, (PAD, rank))


def first_doc(slab_ref, doc_in, term_in, out_ref, near_ref, doc_own, term_own, held, doc_ref, term_ref, arrived):
    copies = [
        pltpu.make_async_copy(term_in, term_ref, arrived.at[2]),
        pltpu.make_async_copy(doc_in, doc_ref, arrived.at[3]),
    ]
    for copy in (*copies, head_copy(slab_ref, near_ref, arrived)):
        copy.start()
    for copy in copies:
        copy.wait()
    tail_copy(slab_ref, held, arrived).start()
    doc_kernel(True, True, slab_ref, near_ref, doc_ref, (term_ref,), out_ref, held, arrived)
    for axis, source, target in ((NEAR, doc_ref, doc_own), (TERM_OWN, term_ref, term_own)):
        rows = target.shape[0]
        start = pl.multiple_of(lax.axis_index(axis) * rows, rows)
        target[...] = source[pl.ds(start, rows), :]


def later_doc(mass, slab_ref, near_ref, doc_ref, *refs):
    *term_refs, out_ref, held, arrived = refs
    doc_kernel(False, mass, slab_ref, near_ref, doc_ref, term_refs, out_ref, held, arrived)


def any_term(last, slab_ref, near_ref, doc_ref, *refs):
    if not last:
        *term_refs, out_ref, held, arrived = refs
        term_kernel(slab_ref, near_ref, doc_ref, term_refs, out_ref, held, arrived)
        return
    *term_refs, out_ref, doc_out, held, arrived = refs
    copy = pltpu.make_async_copy(doc_ref, doc_out, arrived.at[2])
    copy.start()
    term_kernel(slab_ref, near_ref, doc_ref, term_refs, out_ref, held, arrived)
    copy.wait()


WHOLE = pl.BlockSpec(memory_space=pltpu.VMEM)
APART = pl.BlockSpec(memory_space=pltpu.HBM)


def array(*shape):
    return jax.ShapeDtypeStruct(shape, F32)


def call(kernel, arrays, in_specs, outs, out_specs, extra=()):
    slab = arrays[0]
    return pl.pallas_call(
        kernel,
        out_shape=outs,
        in_specs=in_specs,
        out_specs=out_specs,
        scratch_shapes=[
            pltpu.VMEM((slab.shape[0] - HELD, slab.shape[1]), F32),
            *extra,
            pltpu.SemaphoreType.DMA((4,)),
        ],
        compiler_params=pltpu.CompilerParams(vmem_limit_bytes=LIMIT * 2**20),
    )(*arrays)


def on_device(slab, doc_factor, term_factor):
    near = lax.axis_size(NEAR)
    rank = doc_factor.shape[1]
    docs = doc_factor.shape[0] // near
    across = lax.axis_size("y")
    terms = term_factor.shape[0] // (2 * across)
    core, row = (lax.axis_index(axis).astype(jnp.uint32) for axis in ("core", "y"))
    here, away = core * across, (1 - core) * across
    partner = [row ^ at for at in range(across)]
    spots = [at ^ (at >> 1) for at in partner]
    slab, doc_factor, term_factor, core, here, away, partner, spots = lax.optimization_barrier(
        (slab, doc_factor, term_factor, core, here, away, partner, spots)
    )
    term_factor = (term_factor,)
    held = None
    for outer in range(OUTER):
        for inner in range(INNER):
            mass = inner == 0
            blocks = array(near, docs + (PAD if mass else 0), rank)
            if held is None:
                blocks, held, doc_own, term_own = call(
                    first_doc,
                    (slab, *(pltpu.with_memory_space_constraint(factor, pltpu.HBM) for factor in (doc_factor, *term_factor))),
                    [APART] * 3,
                    (blocks, array(HELD, slab.shape[1]), array(docs, rank), array(terms, rank)),
                    (WHOLE,) * 4,
                    [pltpu.VMEM(doc_factor.shape, F32), pltpu.VMEM(term_factor[0].shape, F32)],
                )
            else:
                blocks = call(
                    functools.partial(later_doc, mass),
                    (slab, held, doc_factor, *term_factor),
                    [APART] + [WHOLE] * (2 + len(term_factor)),
                    blocks,
                    WHOLE,
                )
            share = jnp.sum(exchange(blocks, NEAR), axis=0)
            share = total_over(share, FAR)
            if mass:
                term_mass = share[docs]
            doc_own = doc_own * share[:docs] / term_mass
            doc_factor = spread(doc_own, NEAR).reshape(-1, rank)
        last = outer == OUTER - 1
        blocks = array(2 * across, terms + PAD, rank)
        blocks = call(
            functools.partial(any_term, last),
            (slab, held, doc_factor, *term_factor),
            [APART] + [WHOLE] * (2 + len(term_factor)),
            (blocks, array(*doc_factor.shape)) if last else blocks,
            (WHOLE, APART) if last else WHOLE,
        )
        if last:
            blocks, doc_factor = blocks
        mine = lax.dynamic_slice_in_dim(blocks, here, across, 0)
        other = lax.dynamic_slice_in_dim(blocks, away, across, 0)
        mine = mine + swap(other, "core")
        pieces = [lax.dynamic_index_in_dim(mine, at, 0, keepdims=False) for at in partner]
        share = sum([swap(pieces[by], "y", by) for by in SCATTER], pieces[0])
        term_own = term_own * share[:terms] / share[terms]
        pieces = jnp.stack([term_own] + [swap(term_own, "y", by) for by in GATHER])
        mine = jnp.concatenate([lax.dynamic_index_in_dim(pieces, at, 0, keepdims=False) for at in spots], axis=0)
        other = swap(mine, "core")
        term_factor = (mine, other)
    first = core == 0
    term_factor = jnp.concatenate([jnp.where(first, mine, other), jnp.where(first, other, mine)], axis=0)
    return (doc_factor, term_factor)


def solution(mesh):
    parts = Mesh(mesh.devices.reshape(4, 2, 4, 4, 2), ("y", "core", "x", "zh", "zl"))
    return jax.shard_map(
        on_device,
        mesh=parts,
        in_specs=(P(DOC, TERM), P(DOC, None), P(TERM, None)),
        out_specs=(P(DOC, None), P(TERM, None)),
        check_vma=False,
    )
```

```python
import functools

import jax
import jax.numpy as jnp
from jax import lax
from jax.experimental import pallas as pl
from jax.experimental.pallas import tpu as pltpu
from jax.sharding import Mesh, PartitionSpec as P

OUTER = 2
INNER = 2
NEAR = ("zl", "x")
FAR = "zh"
DOC = ("y", "core")
TERM = ("x", "zh", "zl")
TERM_OWN = ("core", "y")
F32 = jnp.float32
PAD = 8
ORDER = (1, 3, 2)
SCATTER = (2, 1, 3)
GATHER = (1, 3, 2)
HELD = 512
DOC_STEP = 256
TERM_STEP = 512
LIMIT = 50


def exchange(blocks, axis):
    return lax.all_to_all(blocks, axis, split_axis=0, concat_axis=0, tiled=True)


def spread(value, axis):
    return exchange(jnp.broadcast_to(value, (lax.axis_size(axis), *value.shape)), axis)


def swap(value, axis, by=1):
    return lax.ppermute(value, axis, [(at, at ^ by) for at in range(lax.axis_size(axis))])


def total_over(value, axis):
    return sum([swap(value, axis, by) for by in ORDER], value)


def halves(value):
    high = value.astype(jnp.bfloat16)
    return high, (value - high.astype(F32)).astype(jnp.bfloat16)


def product_of(doc, term_cat):
    high, low = doc
    return lax.dot_general(
        jnp.concatenate([high, low, high, low], axis=1),
        term_cat,
        (((1,), (1,)), ((), ())),
        preferred_element_type=F32,
    )


def term_operand(term):
    high, low = term
    return jnp.concatenate([high, high, low, low], axis=1)


def head_copy(slab_ref, near_ref, arrived):
    return pltpu.make_async_copy(slab_ref.at[pl.ds(0, HELD)], near_ref, arrived.at[0])


def tail_copy(slab_ref, held, arrived):
    return pltpu.make_async_copy(slab_ref.at[pl.ds(HELD, held.shape[0])], held, arrived.at[1])


def quotients(first, slab_ref, near_ref, docs, term_cat, held, arrived):
    split, step = near_ref.shape[0], docs[0][0].shape[0]
    tail = tail_copy(slab_ref, held, arrived)
    if not first:
        tail.start()
    products = [product_of(doc, term_cat) for doc in docs]
    if first:
        head_copy(slab_ref, near_ref, arrived).wait()
    for at, product in enumerate(products):
        start = at * step
        if start == split:
            tail.wait()
        source = near_ref if start < split else held
        yield halves(source[pl.ds(start % split, step), :] / product)


def loaded(term_refs):
    if len(term_refs) == 1:
        return term_refs[0][...]
    mine, other = (ref[...] for ref in term_refs)
    first = lax.axis_index("core") == 0
    return jnp.concatenate([jnp.where(first, mine, other), jnp.where(first, other, mine)], axis=0)


def doc_blocks(doc_ref, step):
    return [halves(doc_ref[start : start + step, :]) for start in range(0, doc_ref.shape[0], step)]


def doc_kernel(first, mass, slab_ref, near_ref, doc_ref, term_refs, out_ref, held, arrived):
    term_value = loaded(term_refs)
    term = halves(term_value)
    pair = jnp.concatenate(term, axis=1)
    pair = jnp.concatenate([pair, pair], axis=0)
    rank = doc_ref.shape[1]
    rows = out_ref.shape[1] - (PAD if mass else 0)
    docs = doc_blocks(doc_ref, DOC_STEP)
    start = 0
    for quotient in quotients(first, slab_ref, near_ref, docs, term_operand(term), held, arrived):
        both = jnp.dot(jnp.concatenate(quotient, axis=1), pair, preferred_element_type=F32)
        result = both[:, :rank] + both[:, rank:]
        for offset in range(0, DOC_STEP, rows):
            out_ref[(start + offset) // rows, :rows, :] = result[offset : offset + rows, :]
        start += DOC_STEP
    if mass:
        total = jnp.sum(term_value, axis=0, keepdims=True)
        for at in range(out_ref.shape[0]):
            out_ref[at, rows:, :] = jnp.broadcast_to(total, (PAD, rank))


def term_kernel(slab_ref, near_ref, doc_ref, term_refs, out_ref, held, arrived):
    rank = doc_ref.shape[1]
    term_cat = term_operand(halves(loaded(term_refs)))
    docs = doc_blocks(doc_ref, TERM_STEP)
    total = None
    for doc, quotient in zip(docs, quotients(False, slab_ref, near_ref, docs, term_cat, held, arrived)):
        pair = jnp.concatenate(doc, axis=1)
        part = lax.dot_general(
            jnp.concatenate(quotient, axis=0),
            jnp.concatenate([pair, pair], axis=0),
            (((0,), (0,)), ((), ())),
            preferred_element_type=F32,
        )
        total = part if total is None else total + part
    result = total[:, :rank] + total[:, rank:]
    sums = jnp.sum(doc_ref[...], axis=0, keepdims=True)
    count, rows = out_ref.shape[0], out_ref.shape[1] - PAD
    for at in range(count):
        out_ref[at, :rows, :] = result[at * rows : (at + 1) * rows, :]
        out_ref[at, rows:, :] = jnp.broadcast_to(sums, (PAD, rank))


def first_doc(slab_ref, doc_in, term_in, out_ref, near_ref, doc_own, term_own, held, doc_ref, term_ref, arrived):
    copies = [
        pltpu.make_async_copy(term_in, term_ref, arrived.at[2]),
        pltpu.make_async_copy(doc_in, doc_ref, arrived.at[3]),
    ]
    for copy in (*copies, head_copy(slab_ref, near_ref, arrived)):
        copy.start()
    for copy in copies:
        copy.wait()
    tail_copy(slab_ref, held, arrived).start()
    doc_kernel(True, True, slab_ref, near_ref, doc_ref, (term_ref,), out_ref, held, arrived)
    for axis, source, target in ((NEAR, doc_ref, doc_own), (TERM_OWN, term_ref, term_own)):
        rows = target.shape[0]
        start = pl.multiple_of(lax.axis_index(axis) * rows, rows)
        target[...] = source[pl.ds(start, rows), :]


def later_doc(mass, slab_ref, near_ref, doc_ref, *refs):
    *term_refs, out_ref, held, arrived = refs
    doc_kernel(False, mass, slab_ref, near_ref, doc_ref, term_refs, out_ref, held, arrived)


def any_term(last, slab_ref, near_ref, doc_ref, *refs):
    if not last:
        *term_refs, out_ref, held, arrived = refs
        term_kernel(slab_ref, near_ref, doc_ref, term_refs, out_ref, held, arrived)
        return
    *term_refs, out_ref, doc_out, held, arrived = refs
    copy = pltpu.make_async_copy(doc_ref, doc_out, arrived.at[2])
    copy.start()
    term_kernel(slab_ref, near_ref, doc_ref, term_refs, out_ref, held, arrived)
    copy.wait()


WHOLE = pl.BlockSpec(memory_space=pltpu.VMEM)
APART = pl.BlockSpec(memory_space=pltpu.HBM)


def array(*shape):
    return jax.ShapeDtypeStruct(shape, F32)


def call(kernel, arrays, in_specs, outs, out_specs, extra=()):
    slab = arrays[0]
    return pl.pallas_call(
        kernel,
        out_shape=outs,
        in_specs=in_specs,
        out_specs=out_specs,
        scratch_shapes=[
            pltpu.VMEM((slab.shape[0] - HELD, slab.shape[1]), F32),
            *extra,
            pltpu.SemaphoreType.DMA((4,)),
        ],
        compiler_params=pltpu.CompilerParams(vmem_limit_bytes=LIMIT * 2**20),
    )(*arrays)


def on_device(slab, doc_factor, term_factor):
    near = lax.axis_size(NEAR)
    rank = doc_factor.shape[1]
    docs = doc_factor.shape[0] // near
    across = lax.axis_size("y")
    terms = term_factor.shape[0] // (2 * across)
    core, row = (lax.axis_index(axis).astype(jnp.uint32) for axis in ("core", "y"))
    here, away = core * across, (1 - core) * across
    partner = [row ^ at for at in range(across)]
    spots = [at ^ (at >> 1) for at in partner]
    slab, doc_factor, term_factor, core, here, away, partner, spots = lax.optimization_barrier(
        (slab, doc_factor, term_factor, core, here, away, partner, spots)
    )
    term_factor = (term_factor,)
    held = None
    for outer in range(OUTER):
        for inner in range(INNER):
            mass = inner == 0
            blocks = array(near, docs + (PAD if mass else 0), rank)
            if held is None:
                blocks, held, doc_own, term_own = call(
                    first_doc,
                    (slab, *(pltpu.with_memory_space_constraint(factor, pltpu.HBM) for factor in (doc_factor, *term_factor))),
                    [APART] * 3,
                    (blocks, array(HELD, slab.shape[1]), array(docs, rank), array(terms, rank)),
                    (WHOLE,) * 4,
                    [pltpu.VMEM(doc_factor.shape, F32), pltpu.VMEM(term_factor[0].shape, F32)],
                )
            else:
                blocks = call(
                    functools.partial(later_doc, mass),
                    (slab, held, doc_factor, *term_factor),
                    [APART] + [WHOLE] * (2 + len(term_factor)),
                    blocks,
                    WHOLE,
                )
            share = jnp.sum(exchange(blocks, NEAR), axis=0)
            share = total_over(share, FAR)
            if mass:
                term_mass = share[docs]
            doc_own = doc_own * share[:docs] / term_mass
            doc_factor = spread(doc_own, NEAR).reshape(-1, rank)
        last = outer == OUTER - 1
        blocks = array(2 * across, terms + PAD, rank)
        blocks = call(
            functools.partial(any_term, last),
            (slab, held, doc_factor, *term_factor),
            [APART] + [WHOLE] * (2 + len(term_factor)),
            (blocks, array(*doc_factor.shape)) if last else blocks,
            (WHOLE, APART) if last else WHOLE,
        )
        if last:
            blocks, doc_factor = blocks
        mine = lax.dynamic_slice_in_dim(blocks, here, across, 0)
        other = lax.dynamic_slice_in_dim(blocks, away, across, 0)
        mine = mine + swap(other, "core")
        pieces = [lax.dynamic_index_in_dim(mine, at, 0, keepdims=False) for at in partner]
        share = sum([swap(pieces[by], "y", by) for by in SCATTER], pieces[0])
        term_own = term_own * share[:terms] / share[terms]
        pieces = jnp.stack([term_own] + [swap(term_own, "y", by) for by in GATHER])
        mine = jnp.concatenate([lax.dynamic_index_in_dim(pieces, at, 0, keepdims=False) for at in spots], axis=0)
        other = swap(mine, "core")
        term_factor = (mine, other)
    first = core == 0
    term_factor = jnp.concatenate([jnp.where(first, mine, other), jnp.where(first, other, mine)], axis=0)
    return (doc_factor, term_factor)


def solution(mesh):
    parts = Mesh(mesh.devices.reshape(4, 2, 4, 4, 2), ("y", "core", "x", "zh", "zl"))
    return jax.shard_map(
        on_device,
        mesh=parts,
        in_specs=(P(DOC, TERM), P(DOC, None), P(TERM, None)),
        out_specs=(P(DOC, None), P(TERM, None)),
        check_vma=False,
    )
```
